32 devices in a mesh: rows: 16 (over z, y, x), trees: 2 (over core).
Axes of the slice: x: 2, y: 2, z: 4, core: 2. Of those that a mesh axis runs over, the one named last changes fastest.
Arguments:
- tiles: bfloat16 [2, 16, 4, 256, 256], P('trees', 'rows'), may hold values from -0.0625 to 0.0625
- tile_src: int32 [2, 16, 4], P('trees', 'rows'), may hold values from 0 to 3, as said below
- tile_dst: int32 [2, 16, 4], P('trees', 'rows'), may hold values from 0 to 1
- leaf_rhs: bfloat16 [2, 16, 256, 128], P('trees', 'rows'), may hold values from -6 to 6
- leaf_inv: bfloat16 [2, 16, 256, 256], P('trees', 'rows'), may hold values from -0.375 to 0.375
- leaf_owner: int32 [2, 2], P('trees'), may hold values from 0 to 15, as said below
- anc_rhs: bfloat16 [2, 16, 256, 128], P('trees', 'rows'), may hold values from -5 to 5
- anc_inv: bfloat16 [16, 256, 256], P('rows'), may hold values from -0.25 to 0.25
- anc_owner: int32 [4], replicated, may hold values from 0 to 15, as said below
Outputs:
- solved: bfloat16 [4, 256, 128], P(None, None, 'rows')
The draws below stay inside these ranges and needn't reach their ends.
Inputs may be any that keep to these rules, and one draw needn't show every extreme that they name: `leaf_owner`: the 2 owners of one subtree differ. `anc_owner`: all owners differ. `tile_src`: a tile of wave w names a block below 2 * w.
All inputs are finite; a program needn't handle non-finite values.
Results may differ from the reference program's by a relative error of at most 0.011.
Values may be sent and summed in bfloat16 or wider, within the bound.
A program may use at most 64 MiB of HBM per device.

```python
import jax
import jax.numpy as jnp
from jax import lax

B = 256
R = 128
WAVES = 3
WB = 2
TW = 2
TILES = 4
ANC = 4
N_ROWS = 16
N_TREES = 2


def owner_list(key, count):
    order = jax.random.permutation(key, N_ROWS).astype(jnp.int32)
    place = jnp.argmax(order == N_ROWS - 1)
    return jnp.roll(order, -place)[:count]


def draw_leaf_owner(key, part):
    keys = jax.random.split(jax.random.fold_in(key, 11), N_TREES)
    return jax.vmap(lambda k: owner_list(k, WB))(keys)


def draw_anc_owner(key, part):
    return owner_list(jax.random.fold_in(key, 12), ANC)


def draw_tile_src(key, part):
    waves = jnp.arange(TILES, dtype=jnp.int32) // TW + 1
    limit = jnp.broadcast_to(WB * waves, (N_TREES, N_ROWS, TILES))
    values = jax.random.randint(jax.random.fold_in(key, 13), (N_TREES, N_ROWS, TILES), 0, limit).astype(jnp.int32)
    values = values.at[0, 0, 0].set(0)
    return values.at[0, 0, TILES - 1].set(WB * (WAVES - 1) - 1)


def draw_tile_dst(key, part):
    values = jax.random.randint(jax.random.fold_in(key, 14), (N_TREES, N_ROWS, TILES), 0, WB).astype(jnp.int32)
    values = values.at[0, 0, 0].set(0)
    return values.at[0, 0, TILES - 1].set(WB - 1)


def level_of(stream_key, shape, pieces, least, largest):
    def one(dim, shards_of):
        draws = jax.random.uniform(jax.random.fold_in(jax.random.fold_in(stream_key, 6), dim), (shards_of,), jnp.float32, least / len(pieces), largest / len(pieces))
        return jnp.repeat(jnp.exp(draws), shape[dim] // shards_of).reshape((-1,) + (1,) * (len(shape) - dim - 1))

    loudness = one(*pieces[0])
    for cut in pieces[1:]:
        loudness = loudness * one(*cut)
    return loudness


def normal_values(rng, dims, spread, reach, shards=(), kind=jnp.bfloat16):
    result = spread * jax.random.normal(rng, dims, jnp.float32)
    if shards:
        result = result * level_of(rng, dims, shards, -0.22, 0.18)
    return jnp.clip(result, -reach, reach).astype(kind)


def setup_inputs(seed: int = 0) -> dict:
    key_of = jax.random.split(jax.random.key(seed), 10)
    tiles = normal_values(key_of[0], (N_TREES, N_ROWS, TILES, B, B), (B * N_TREES * N_ROWS * TW // WB) ** -0.5, 0.0625, ((0, 2), (1, 16)))
    tile_src = draw_tile_src(jax.random.fold_in(key_of[9], 71), 0)
    tile_dst = draw_tile_dst(jax.random.fold_in(key_of[9], 71), 0)
    leaf_rhs = normal_values(key_of[3], (N_TREES, N_ROWS, B, R), 1.0, 6.0, ((0, 2), (1, 16)))
    leaf_inv = normal_values(key_of[4], (N_TREES, N_ROWS, B, B), B ** -0.5, 0.375, ((0, 2), (1, 16)))
    leaf_owner = draw_leaf_owner(jax.random.fold_in(key_of[9], 71), 0)
    anc_rhs = normal_values(key_of[6], (N_TREES, N_ROWS, B, R), 0.35, 5.0, ((0, 2), (1, 16)))
    anc_inv = normal_values(key_of[7], (N_ROWS, B, B), (2 * B) ** -0.5, 0.25, ((0, 16),))
    anc_owner = draw_anc_owner(jax.random.fold_in(key_of[9], 71), 0)
    return dict(tiles=tiles, tile_src=tile_src, tile_dst=tile_dst, leaf_rhs=leaf_rhs, leaf_inv=leaf_inv, leaf_owner=leaf_owner, anc_rhs=anc_rhs, anc_inv=anc_inv, anc_owner=anc_owner)


def reference(tiles, tile_src, tile_dst, leaf_rhs, leaf_inv, leaf_owner, anc_rhs, anc_inv, anc_owner):
    def leaf_solve(tree):
        blocks = []
        for block in range(WB):
            owner = leaf_owner[tree, block]
            blocks.append(jnp.dot(leaf_inv[tree, owner], leaf_rhs[tree, owner], preferred_element_type=jnp.float32).astype(jnp.bfloat16))
        return jnp.stack(blocks)

    leaf_x = lax.map(leaf_solve, jnp.arange(N_TREES, dtype=jnp.int32))
    solved = []
    for wave in range(1, WAVES):
        start = (wave - 1) * TW
        prior = jnp.stack(solved) if len(solved) > 0 else None

        def add_device(carry, index):
            tree = index // N_ROWS
            row = index % N_ROWS
            sources = leaf_x[tree]
            if prior is not None:
                sources = jnp.concatenate([sources, prior], 0)
            block_tiles = lax.dynamic_slice_in_dim(tiles[tree, row], start, TW, 0)
            src = lax.dynamic_slice_in_dim(tile_src[tree, row], start, TW, 0)
            dst = lax.dynamic_slice_in_dim(tile_dst[tree, row], start, TW, 0)
            picked = jnp.take(sources, src, axis=0)
            product = jnp.einsum("kij,kjr->kir", block_tiles.astype(jnp.float32), picked.astype(jnp.float32))
            onehot = (dst[:, None] == jnp.arange(WB, dtype=jnp.int32)[None, :]).astype(jnp.float32)
            return carry + jnp.einsum("kb,kir->bir", onehot, product), None

        update, unused = lax.scan(add_device, jnp.zeros((WB, B, R), jnp.float32), jnp.arange(N_TREES * N_ROWS, dtype=jnp.int32))
        for block in range(WB):
            owner = anc_owner[(wave - 1) * WB + block]
            shares = jnp.sum(anc_rhs[:, owner].astype(jnp.float32), axis=0)
            target = (shares - update[block]).astype(jnp.bfloat16)
            solved.append(jnp.dot(anc_inv[owner], target, preferred_element_type=jnp.float32).astype(jnp.bfloat16))
    return jnp.stack(solved)
```

```python
import functools

import jax
import jax.numpy as jnp
from jax import lax
from jax.experimental import pallas as pl
from jax.experimental.pallas import tpu as pltpu
from jax.sharding import PartitionSpec as P

WAVES = 3
WB = 2
TW = 2
MESH = pl.DeviceIdType.MESH
F32 = jnp.float32
BF16 = jnp.bfloat16


def broadcast(block, axis, source):
    block = jnp.where(lax.axis_index(axis) == source, block, jnp.zeros_like(block))
    return lax.psum(block, axis)


def general_body(tiles, tile_src, tile_dst, leaf_rhs, leaf_inv, leaf_owner, anc_rhs, anc_inv, anc_owner):
    row_count = lax.axis_size("rows")
    here = lax.axis_index("rows")
    share = leaf_rhs.shape[-1] // row_count
    own_leaf = jnp.dot(leaf_inv[0, 0], leaf_rhs[0, 0], preferred_element_type=F32).astype(BF16)
    known = []
    for block in range(WB):
        known.append(broadcast(own_leaf, "rows", leaf_owner[0, block]))
    outputs = []
    for wave in range(1, WAVES):
        start = (wave - 1) * TW
        sources = jnp.stack(known)
        block_tiles = tiles[0, 0, start : start + TW]
        picked = jnp.take(sources, tile_src[0, 0, start : start + TW], axis=0)
        product = jnp.einsum("kij,kjr->kir", block_tiles, picked, preferred_element_type=F32)
        onehot = (
            tile_dst[0, 0, start : start + TW][:, None] == jnp.arange(WB, dtype=jnp.int32)[None, :]
        ).astype(F32)
        owners = anc_owner[(wave - 1) * WB : wave * WB]
        mine = (owners == here).astype(F32)
        partial_value = mine[:, None, None] * anc_rhs[0, 0].astype(F32)[None] - jnp.einsum(
            "kb,kir->bir", onehot, product
        )
        summed = lax.psum(partial_value, ("rows", "trees"))
        chosen = jnp.einsum("b,bir->ir", mine, summed).astype(BF16)
        local_x = jnp.dot(anc_inv[0], chosen, preferred_element_type=F32).astype(BF16)
        for block in range(WB):
            result = broadcast(local_x, "rows", owners[block])
            known.append(result)
            outputs.append(lax.dynamic_slice_in_dim(result, here * share, share, 1))
    return jnp.stack(outputs)


NT = (((1,), (1,)), ((), ()))


def kernel(
    n, nt, tiles_h, src, dst, rhs_h, linv_h, lown, arhs_h, ainv_h, aown, out,
    tiles, rhs, linv, arhs, ainv, own, leaf_rs, leaf_ag, inv_rs, inv_half, inv_ag, known, u_send, u_recv, xs,
    u_mine, u_other, coef, coef_rs, mat_rs, mat_send, mat_recv, mat_sum, mat_ag, lsem, ssem, rsem,
):
    r = lax.axis_index("rows")
    t = lax.axis_index("trees")
    depth = rhs.shape[0]
    count = rhs.shape[1]
    ch = depth // n
    share = count // n
    every = n * nt

    def partner(m):
        if n & (n - 1):
            return lax.rem(r + m, n)
        j = r
        bit = 1
        while bit < n:
            if m & bit:
                j = j + bit * (1 - 2 * lax.rem(r // bit, 2))
            bit *= 2
        return j

    inner = 1
    while inner * inner * 4 <= n and n % (inner * 2) == 0:
        inner *= 2
    masks = sorted(range(1, n), key=lambda m: (-(m // inner + m % inner), m // inner))
    others = [partner(m) for m in masks]
    everyone = [(j, q) for j in others for q in (t, 1 - t)] + [(r, 1 - t)]

    barrier = pltpu.get_barrier_semaphore()
    for where in everyone:
        pl.semaphore_signal(barrier, inc=1, device_id=where, device_id_type=MESH)

    loads = []
    for i, (a, b) in enumerate(
        ((linv_h.at[0, 0], linv), (rhs_h.at[0, 0], rhs), (ainv_h.at[0], ainv), (arhs_h.at[0, 0], arhs), (tiles_h.at[0, 0], tiles))
    ):
        c = pltpu.make_async_copy(a, b, lsem.at[i])
        c.start()
        loads.append(c)
    for k in range(TW):
        for b in range(WB):
            for s in range(WB):
                hit = (dst[0, 0, TW + k] == b) & (src[0, 0, TW + k] == WB + s)
                coef[(k * WB + b) * WB + s] = jnp.full((128,), jnp.where(hit, 1.0, 0.0), F32)
    loads[0].wait()
    loads[1].wait()
    own_leaf = jnp.dot(linv[...], rhs[...], preferred_element_type=F32)
    own[...] = own_leaf.T.astype(BF16).reshape(n, share, depth)
    loads[2].wait()
    loads[4].wait()
    pl.semaphore_wait(barrier, every - 1)

    def push(phase, a, b, where):
        pltpu.make_async_remote_copy(
            src_ref=a, dst_ref=b, send_sem=ssem.at[phase], recv_sem=rsem.at[phase],
            device_id=where, device_id_type=MESH,
        ).start()

    def rows_send(phase, make):
        for j in others:
            push(phase, *make(j), (j, t))

    def landed(phase, view):
        pltpu.make_async_copy(view, view, rsem.at[phase]).wait()

    def sent(phase, view):
        pltpu.make_async_copy(view, view, ssem.at[phase]).wait()

    most = pl.ds(0, n - 1)
    outer = n // inner
    ro, ri = r // inner, lax.rem(r, inner)
    chunk = ri * outer + ro
    lanes_each = depth // nt
    lanes = pl.ds(pl.multiple_of(t * lanes_each, lanes_each), lanes_each)

    def rows_of(at):
        return pl.ds(pl.multiple_of(at * ch, ch), ch)

    def inv_part(j):
        return rows_of(lax.rem(j, inner) * outer + j // inner)

    def inner_send(w):
        held = pl.ds(ri * outer, outer)
        for k in range(1, inner):
            to = ro * inner + lax.rem(ri + k, inner)
            push(INV_IN + w, inv_ag.at[w, held], inv_ag.at[w, held], (to, t))

    inner_view = inv_ag.at[0, pl.ds(0, (inner - 1) * outer)]
    outer_view = inv_ag.at[0, pl.ds(0, (outer - 1) * (WAVES - 1))]
    (LEAF_RS, INV_RS, LEAF_AG, INV_OUT, INV_SWAP, COEF, MAT_RS, MAT_ZRS, MAT_ZAG, MAT_AG, X1, X2, INV_IN, _,
     UP, _, US, _) = range(18)
    zs = [lax.rem(ro + k, outer) for k in range(1, outer)]
    near = [(lax.rem(ri + k, inner), q) for k in range(1, inner) for q in (t, 1 - t)] + [(ri, 1 - t)]
    place = ri * nt + t
    part = depth // (inner * nt)
    piece = part // outer
    rows_send(LEAF_RS, lambda j: (own.at[j], leaf_rs.at[r]))
    leaf_rs[r] = own[r]
    second = pl.ds(TW, TW)

    def mat_rows(i, q):
        return pl.ds(pl.multiple_of((i * nt + q) * part, part), part)

    for i, q in near:
        push(COEF, coef, coef_rs.at[place], (ro * inner + i, q))
        push(MAT_RS, tiles.at[second, mat_rows(i, q)], mat_rs.at[place], (ro * inner + i, q))
    coef_rs[place] = coef[...]
    mat_rs[place] = tiles[second, mat_rows(ri, t)]
    rows_send(INV_RS, lambda j: (ainv.at[inv_part(j), lanes], inv_rs.at[r]))
    inv_rs[r] = ainv[inv_part(r), lanes]

    landed(LEAF_RS, leaf_rs.at[most])
    for b in range(WB):
        leaf_ag[r, b] = leaf_rs[lown[0, b]]
    rows_send(LEAF_AG, lambda j: (leaf_ag.at[r], leaf_ag.at[r]))

    landed(COEF, coef_rs.at[pl.ds(0, inner * nt - 1)])
    landed(MAT_RS, mat_rs.at[pl.ds(0, inner * nt - 1)])
    slots = [[jnp.zeros((part, depth), F32) for s in range(WB)] for b in range(WB)]
    for j in range(inner * nt):
        for k in range(TW):
            value = mat_rs[j, k].astype(F32)
            for b in range(WB):
                for s in range(WB):
                    at = (k * WB + b) * WB + s
                    scale = coef_rs[j, at : at + 1]
                    scale = jnp.concatenate([scale] * (depth // 128), axis=1)
                    slots[b][s] = slots[b][s] + scale * value
    for b in range(WB):
        for s in range(WB):
            mat_send[:, b, s] = slots[b][s].reshape(outer, piece, depth).astype(BF16)
    for z in zs:
        push(MAT_ZRS, mat_send.at[z], mat_recv.at[ro], (z * inner + ri, t))
    mat_recv[ro] = mat_send[ro]

    landed(INV_RS, inv_rs.at[most])
    for w in range(WAVES - 1):
        inv_half[w] = inv_rs[aown[w * WB + 1 - t]]
        push(INV_SWAP, inv_half.at[w], inv_ag.at[w, chunk, :, lanes], (r, 1 - t))
    for w in range(WAVES - 1):
        inv_ag[w, chunk, :, lanes] = inv_rs[aown[w * WB + t]]
    loads[3].wait()
    arhs_t = arhs[...].astype(F32).T
    landed(INV_SWAP, inv_half)
    for z in zs:
        for w in range(WAVES - 1):
            push(INV_OUT, inv_ag.at[w, chunk], inv_ag.at[w, chunk], (z * inner + ri, t))

    landed(MAT_ZRS, mat_recv.at[pl.ds(0, outer - 1)])
    mat_sum[:, ro] = jnp.sum(mat_recv[...].astype(F32), axis=0).astype(BF16)
    for z in zs:
        push(MAT_ZAG, mat_sum.at[:, ro], mat_sum.at[:, ro], (z * inner + ri, t))

    landed(LEAF_AG, leaf_ag.at[most])
    for b in range(WB):
        known[b] = leaf_ag[:, b].reshape(count, depth)
    for w in range(WAVES - 1):
        products = []
        for k in range(w * TW, (w + 1) * TW):
            from_leaf = known[jnp.minimum(src[0, 0, k], WB - 1)]
            products.append(lax.dot_general(from_leaf, tiles[k], NT, preferred_element_type=F32))
        for b in range(WB):
            u = jnp.where(aown[w * WB + b] == r, arhs_t, 0.0)
            for k in range(TW):
                hit = (dst[0, 0, w * TW + k] == b) & (src[0, 0, w * TW + k] < WB)
                u = u - jnp.where(hit, products[k], 0.0)
            u_mine[w, b] = u.astype(BF16)
        push(US + w, u_mine.at[w, 1 - t], u_other.at[w], (r, 1 - t))
    landed(INV_OUT, outer_view)
    inner_send(0)
    for w in range(WAVES - 1):
        landed(US + w, u_other.at[w])
        u = u_mine[w, t].astype(F32) + u_other[w].astype(F32)
        u_send[w] = u.reshape(n, share, depth).astype(BF16)
        rows_send(UP + w, lambda j: (u_send.at[w, j], u_recv.at[w, r]))
        u_recv[w, r] = u_send[w, r]
    landed(MAT_ZAG, mat_sum.at[:, pl.ds(0, outer - 1)])
    for i, q in near:
        push(MAT_AG, mat_sum.at[q], mat_ag.at[place], (ro * inner + i, q))
    mat_ag[place] = mat_sum[t]
    inner_send(1)

    def solve(w, y):
        inv = inv_ag[w].reshape(depth, depth)
        xs[w, t] = lax.dot_general(y.astype(BF16), inv, NT, preferred_element_type=F32).astype(BF16)
        push(X1 + w, xs.at[w, t], xs.at[w, t], (r, 1 - t))

    landed(UP, u_recv.at[0, most])
    y = jnp.sum(u_recv[0].astype(F32), axis=0)
    landed(INV_IN, inner_view)
    solve(0, y)
    landed(UP + 1, u_recv.at[1, most])
    y = jnp.sum(u_recv[1].astype(F32), axis=0)
    landed(MAT_AG, mat_ag.at[pl.ds(0, inner * nt - 1)])
    landed(INV_IN + 1, inner_view)
    landed(X1, xs.at[0, 0])
    for s in range(WB):
        mat = mat_ag[:, :, s].reshape(depth, depth)
        y = y - lax.dot_general(xs[0, s], mat, NT, preferred_element_type=F32)
    solve(1, y)
    landed(X2, xs.at[0, 0])
    for w in range(WAVES - 1):
        for b in range(WB):
            out[w * WB + b] = xs[w, b]

    sent(LEAF_RS, own.at[most])
    sent(INV_RS, inv_rs.at[most])
    sent(COEF, coef_rs.at[pl.ds(0, inner * nt - 1)])
    sent(MAT_RS, mat_rs.at[pl.ds(0, inner * nt - 1)])
    sent(LEAF_AG, leaf_ag.at[most])
    sent(INV_OUT, outer_view)
    sent(INV_SWAP, inv_half)
    sent(MAT_ZRS, mat_recv.at[pl.ds(0, outer - 1)])
    sent(MAT_ZAG, mat_sum.at[:, pl.ds(0, outer - 1)])
    sent(MAT_AG, mat_ag.at[pl.ds(0, inner * nt - 1)])
    for w in range(WAVES - 1):
        sent(US + w, u_other.at[w])
        sent(UP + w, u_recv.at[w, most])
        sent(INV_IN + w, inner_view)
        sent(X1 + w, xs.at[0, 0])


def fast_body(n, nt, tiles, tile_src, tile_dst, leaf_rhs, leaf_inv, leaf_owner, anc_rhs, anc_inv, anc_owner):
    depth, count = leaf_rhs.shape[-2:]
    kinds = tiles.shape[2]
    ch, share, every = depth // n, count // n, n * nt
    waves = WAVES - 1
    inner = 1
    while inner * inner * 4 <= n and n % (inner * 2) == 0:
        inner *= 2
    outer, part = n // inner, depth // (inner * nt)
    phases = 18
    any_spec = pl.BlockSpec(memory_space=pl.ANY)
    smem = pl.BlockSpec(memory_space=pltpu.SMEM)
    found = pl.pallas_call(
        functools.partial(kernel, n, nt),
        out_shape=jax.ShapeDtypeStruct((waves * WB, share, depth), BF16),
        in_specs=[any_spec, smem, smem, any_spec, any_spec, smem, any_spec, any_spec, smem],
        out_specs=pl.BlockSpec(memory_space=pltpu.VMEM),
        scratch_shapes=[
            pltpu.VMEM((kinds, depth, depth), BF16),
            pltpu.VMEM((depth, count), BF16),
            pltpu.VMEM((depth, depth), BF16),
            pltpu.VMEM((depth, count), BF16),
            pltpu.VMEM((depth, depth), BF16),
            pltpu.VMEM((n, share, depth), BF16),
            pltpu.VMEM((n, share, depth), BF16),
            pltpu.VMEM((n, WB, share, depth), BF16),
            pltpu.VMEM((n, ch, depth // nt), BF16),
            pltpu.VMEM((waves, ch, depth // nt), BF16),
            pltpu.VMEM((waves, n, ch, depth), BF16),
            pltpu.VMEM((WB * waves, count, depth), BF16),
            pltpu.VMEM((waves, n, share, depth), BF16),
            pltpu.VMEM((waves, n, share, depth), BF16),
            pltpu.VMEM((waves, WB, share, depth), BF16),
            pltpu.VMEM((waves, WB, count, depth), BF16),
            pltpu.VMEM((waves, count, depth), BF16),
            pltpu.VMEM((TW * WB * WB, 128), F32),
            pltpu.VMEM((inner * nt, TW * WB * WB, 128), F32),
            pltpu.VMEM((inner * nt, TW, part, depth), BF16),
            pltpu.VMEM((outer, WB, WB, part // outer, depth), BF16),
            pltpu.VMEM((outer, WB, WB, part // outer, depth), BF16),
            pltpu.VMEM((WB, outer, WB, part // outer, depth), BF16),
            pltpu.VMEM((inner * nt, outer, WB, part // outer, depth), BF16),
            pltpu.SemaphoreType.DMA((5,)),
            pltpu.SemaphoreType.DMA((phases,)),
            pltpu.SemaphoreType.DMA((phases,)),
        ],
        compiler_params=pltpu.CompilerParams(collective_id=0, has_side_effects=True),
    )(tiles, tile_src, tile_dst, leaf_rhs, leaf_inv, leaf_owner, anc_rhs, anc_inv, anc_owner)
    return jnp.swapaxes(found, 1, 2)


def solution(mesh):
    n, nt = mesh.shape["rows"], mesh.shape["trees"]
    placed = (
        P("trees", "rows", None, None, None),
        P("trees", "rows", None),
        P("trees", "rows", None),
        P("trees", "rows", None, None),
        P("trees", "rows", None, None),
        P("trees", None),
        P("trees", "rows", None, None),
        P("rows", None, None),
        P(),
    )

    def body(*args):
        depth, count = args[3].shape[-2:]
        if WAVES == 3 and nt == WB and n > 3 and depth % (16 * n) == 0 and depth % (128 * nt) == 0 and count % (8 * n) == 0:
            return fast_body(n, nt, *args)
        return general_body(*args)

    return jax.shard_map(
        body, mesh=mesh, in_specs=placed, out_specs=P(None, None, "rows"), check_vma=False
    )
```

```python
import functools

import jax
import jax.numpy as jnp
from jax import lax
from jax.experimental import pallas as pl
from jax.experimental.pallas import tpu as pltpu
from jax.sharding import PartitionSpec as P

WAVES = 3
WB = 2
TW = 2
MESH = pl.DeviceIdType.MESH
F32 = jnp.float32
BF16 = jnp.bfloat16


def broadcast(block, axis, source):
    block = jnp.where(lax.axis_index(axis) == source, block, jnp.zeros_like(block))
    return lax.psum(block, axis)


def general_body(tiles, tile_src, tile_dst, leaf_rhs, leaf_inv, leaf_owner, anc_rhs, anc_inv, anc_owner):
    row_count = lax.axis_size("rows")
    here = lax.axis_index("rows")
    share = leaf_rhs.shape[-1] // row_count
    own_leaf = jnp.dot(leaf_inv[0, 0], leaf_rhs[0, 0], preferred_element_type=F32).astype(BF16)
    known = []
    for block in range(WB):
        known.append(broadcast(own_leaf, "rows", leaf_owner[0, block]))
    outputs = []
    for wave in range(1, WAVES):
        start = (wave - 1) * TW
        sources = jnp.stack(known)
        block_tiles = tiles[0, 0, start : start + TW]
        picked = jnp.take(sources, tile_src[0, 0, start : start + TW], axis=0)
        product = jnp.einsum("kij,kjr->kir", block_tiles, picked, preferred_element_type=F32)
        onehot = (
            tile_dst[0, 0, start : start + TW][:, None] == jnp.arange(WB, dtype=jnp.int32)[None, :]
        ).astype(F32)
        owners = anc_owner[(wave - 1) * WB : wave * WB]
        mine = (owners == here).astype(F32)
        partial_value = mine[:, None, None] * anc_rhs[0, 0].astype(F32)[None] - jnp.einsum(
            "kb,kir->bir", onehot, product
        )
        summed = lax.psum(partial_value, ("rows", "trees"))
        chosen = jnp.einsum("b,bir->ir", mine, summed).astype(BF16)
        local_x = jnp.dot(anc_inv[0], chosen, preferred_element_type=F32).astype(BF16)
        for block in range(WB):
            result = broadcast(local_x, "rows", owners[block])
            known.append(result)
            outputs.append(lax.dynamic_slice_in_dim(result, here * share, share, 1))
    return jnp.stack(outputs)


NT = (((1,), (1,)), ((), ()))


def kernel(
    n, nt, tiles_h, src, dst, rhs_h, linv_h, lown, arhs_h, ainv_h, aown, out,
    tiles, rhs, linv, arhs, ainv, own, leaf_rs, leaf_ag, inv_half, inv_ag, known, u_send, u_recv, xs,
    u_mine, u_other, mat_src, mat_rs, mat_send, mat_recv, mat_sum, mat_ag, lsem, ssem, rsem,
):
    r = lax.axis_index("rows")
    t = lax.axis_index("trees")
    depth = rhs.shape[0]
    count = rhs.shape[1]
    ch = depth // n
    share = count // n
    every = n * nt

    def partner(m):
        if n & (n - 1):
            return lax.rem(r + m, n)
        j = r
        bit = 1
        while bit < n:
            if m & bit:
                j = j + bit * (1 - 2 * lax.rem(r // bit, 2))
            bit *= 2
        return j

    inner = 1
    while inner * inner * 4 <= n and n % (inner * 2) == 0:
        inner *= 2
    masks = sorted(range(1, n), key=lambda m: (-(m // inner + m % inner), m // inner))
    others = [partner(m) for m in masks]
    everyone = [(j, q) for j in others for q in (t, 1 - t)] + [(r, 1 - t)]

    barrier = pltpu.get_barrier_semaphore()
    for where in everyone:
        pl.semaphore_signal(barrier, inc=1, device_id=where, device_id_type=MESH)

    loads = []
    for i, (a, b) in enumerate(
        ((linv_h.at[0, 0], linv), (rhs_h.at[0, 0], rhs), (ainv_h.at[0], ainv), (arhs_h.at[0, 0], arhs), (tiles_h.at[0, 0], tiles))
    ):
        c = pltpu.make_async_copy(a, b, lsem.at[i])
        c.start()
        loads.append(c)
    coef = []
    for k in range(TW):
        for b in range(WB):
            for s in range(WB):
                hit = (dst[0, 0, TW + k] == b) & (src[0, 0, TW + k] == WB + s)
                coef.append(jnp.full((1, depth), jnp.where(hit, 1.0, 0.0), F32))
    coef = jnp.concatenate(coef, axis=0).astype(BF16)
    loads[0].wait()
    loads[1].wait()
    own_leaf = jnp.dot(linv[...], rhs[...], preferred_element_type=F32)
    own[:, :share] = own_leaf.T.astype(BF16).reshape(n, share, depth)
    loads[2].wait()
    half, width = ch // nt, depth // nt
    lanes0 = pl.ds(pl.multiple_of(t * width, width), width)
    mine = ainv[:, lanes0]
    for j in range(n):
        at = (j % inner) * (n // inner) + j // inner
        for q in range(nt):
            own[j, share:, q * width : (q + 1) * width] = mine[at * ch + q * half : at * ch + (q + 1) * half]
    loads[4].wait()
    pieces = inner * nt
    part = depth // pieces
    for j in range(pieces):
        for k in range(TW):
            mat_src[j, k * part : (k + 1) * part] = tiles[TW + k, j * part : (j + 1) * part]
        mat_src[j, TW * part :] = coef
    pl.semaphore_wait(barrier, every - 1)

    def push(phase, a, b, where):
        pltpu.make_async_remote_copy(
            src_ref=a, dst_ref=b, send_sem=ssem.at[phase], recv_sem=rsem.at[phase],
            device_id=where, device_id_type=MESH,
        ).start()

    def rows_send(phase, make):
        for j in others:
            push(phase, *make(j), (j, t))

    def landed(phase, view):
        pltpu.make_async_copy(view, view, rsem.at[phase]).wait()

    def sent(phase, view):
        pltpu.make_async_copy(view, view, ssem.at[phase]).wait()

    most = pl.ds(0, n - 1)
    outer = n // inner
    ro, ri = r // inner, lax.rem(r, inner)
    chunk = ri * outer + ro
    lanes_each = depth // nt
    lanes = pl.ds(pl.multiple_of(t * lanes_each, lanes_each), lanes_each)

    def rows_of(at):
        return pl.ds(pl.multiple_of(at * ch, ch), ch)

    def inv_part(j):
        return rows_of(lax.rem(j, inner) * outer + j // inner)

    inner_view = inv_ag.at[:, pl.ds(0, (inner - 1) * outer)]
    outer_view = inv_ag.at[0, pl.ds(0, outer * nt - 1)]
    (LEAF_RS, INV_RS, LEAF_AG, INV_OUT, _, INV_SWAP, COEF, MAT_RS, MAT_ZRS, MAT_ZAG, MAT_AG, X1, X2, INV_IN, _,
     UP, _, US, _) = range(19)
    zs = [lax.rem(ro + k, outer) for k in range(1, outer)]
    near = [(lax.rem(ri + k, inner), q) for k in range(1, inner) for q in (t, 1 - t)] + [(ri, 1 - t)]
    place = ri * nt + t
    part = depth // (inner * nt)
    piece = part // outer
    rows_send(LEAF_RS, lambda j: (own.at[j], leaf_rs.at[r]))
    leaf_rs[r] = own[r]
    for i, q in near:
        push(MAT_RS, mat_src.at[i * nt + q], mat_rs.at[place], (ro * inner + i, q))
    mat_rs[place] = mat_src[place]
    landed(LEAF_RS, leaf_rs.at[most])
    for b in range(WB):
        leaf_ag[r, b] = leaf_rs[lown[0, b], :share]
    rows_send(LEAF_AG, lambda j: (leaf_ag.at[r], leaf_ag.at[r]))

    def picked(owner):
        rows = leaf_rs[owner, share:]
        return jnp.concatenate([rows[:, q * lanes_each : (q + 1) * lanes_each] for q in range(nt)], axis=0)

    for b in range(WB):
        for w in range(WAVES - 1):
            inv_half[b, w] = picked(aown[w * WB + b])
    for z in zs:
        for q in (t, 1 - t):
            push(INV_OUT, inv_half.at[q], inv_ag.at[:, chunk, :, lanes], (z * inner + ri, q))
    push(INV_OUT, inv_half.at[1 - t], inv_ag.at[:, chunk, :, lanes], (r, 1 - t))
    inv_ag[:, chunk, :, lanes] = inv_half[t]
    landed(MAT_RS, mat_rs.at[pl.ds(0, inner * nt - 1)])
    slots = [[jnp.zeros((part, depth), F32) for s in range(WB)] for b in range(WB)]
    for j in range(inner * nt):
        scales = mat_rs[j, TW * part :].astype(F32)
        for k in range(TW):
            value = mat_rs[j, k * part : (k + 1) * part].astype(F32)
            for b in range(WB):
                for s in range(WB):
                    at = (k * WB + b) * WB + s
                    slots[b][s] = slots[b][s] + scales[at : at + 1] * value
    for b in range(WB):
        for s in range(WB):
            mat_send[:, b, s] = slots[b][s].reshape(outer, piece, depth).astype(BF16)
    for z in zs:
        push(MAT_ZRS, mat_send.at[z], mat_recv.at[ro], (z * inner + ri, t))
    mat_recv[ro] = mat_send[ro]

    loads[3].wait()
    arhs_t = arhs[...].astype(F32).T
    landed(MAT_ZRS, mat_recv.at[pl.ds(0, outer - 1)])
    mat_sum[:, ro] = jnp.sum(mat_recv[...].astype(F32), axis=0).astype(BF16)
    for z in zs:
        push(MAT_ZAG, mat_sum.at[:, ro], mat_sum.at[:, ro], (z * inner + ri, t))

    landed(INV_OUT, outer_view)
    held = pl.ds(ri * outer, outer)
    for k in range(1, inner):
        to = ro * inner + lax.rem(ri + k, inner)
        push(INV_IN, inv_ag.at[:, held], inv_ag.at[:, held], (to, t))
    landed(LEAF_AG, leaf_ag.at[most])
    for b in range(WB):
        known[b] = leaf_ag[:, b].reshape(count, depth)
    for w in (0,):
        products = []
        for k in range(w * TW, (w + 1) * TW):
            from_leaf = known[jnp.minimum(src[0, 0, k], WB - 1)]
            products.append(lax.dot_general(from_leaf, tiles[k], NT, preferred_element_type=F32))
        for b in range(WB):
            u = jnp.where(aown[w * WB + b] == r, arhs_t, 0.0)
            for k in range(TW):
                hit = (dst[0, 0, w * TW + k] == b) & (src[0, 0, w * TW + k] < WB)
                u = u - jnp.where(hit, products[k], 0.0)
            u_mine[w, b] = u.astype(BF16)
        push(US + w, u_mine.at[w, 1 - t], u_other.at[w], (r, 1 - t))
    for w in (1,):
        products = []
        for k in range(w * TW, (w + 1) * TW):
            from_leaf = known[jnp.minimum(src[0, 0, k], WB - 1)]
            products.append(lax.dot_general(from_leaf, tiles[k], NT, preferred_element_type=F32))
        for b in range(WB):
            u = jnp.where(aown[w * WB + b] == r, arhs_t, 0.0)
            for k in range(TW):
                hit = (dst[0, 0, w * TW + k] == b) & (src[0, 0, w * TW + k] < WB)
                u = u - jnp.where(hit, products[k], 0.0)
            u_mine[w, b] = u.astype(BF16)
        push(US + w, u_mine.at[w, 1 - t], u_other.at[w], (r, 1 - t))
    for w in (0,):
        landed(US + w, u_other.at[w])
        u = u_mine[w, t].astype(F32) + u_other[w].astype(F32)
        u_send[w] = u.reshape(n, share, depth).astype(BF16)
        rows_send(UP + w, lambda j: (u_send.at[w, j], u_recv.at[w, r]))
        u_recv[w, r] = u_send[w, r]
    for w in (1,):
        landed(US + w, u_other.at[w])
        u = u_mine[w, t].astype(F32) + u_other[w].astype(F32)
        u_send[w] = u.reshape(n, share, depth).astype(BF16)
        rows_send(UP + w, lambda j: (u_send.at[w, j], u_recv.at[w, r]))
        u_recv[w, r] = u_send[w, r]
    landed(MAT_ZAG, mat_sum.at[:, pl.ds(0, outer - 1)])
    for i, q in near:
        push(MAT_AG, mat_sum.at[q], mat_ag.at[place], (ro * inner + i, q))
    mat_ag[place] = mat_sum[t]
    def solve(w, y):
        inv = inv_ag[w].reshape(depth, depth)
        xs[w, t] = lax.dot_general(y.astype(BF16), inv, NT, preferred_element_type=F32).astype(BF16)
        push(X1 + w, xs.at[w, t], xs.at[w, t], (r, 1 - t))

    landed(UP, u_recv.at[0, most])
    y = jnp.sum(u_recv[0].astype(F32), axis=0)
    landed(INV_IN, inner_view)
    solve(0, y)
    landed(UP + 1, u_recv.at[1, most])
    y = jnp.sum(u_recv[1].astype(F32), axis=0)
    landed(MAT_AG, mat_ag.at[pl.ds(0, inner * nt - 1)])
    landed(X1, xs.at[0, 0])
    for s in range(WB):
        mat = mat_ag[:, :, s].reshape(depth, depth)
        y = y - lax.dot_general(xs[0, s], mat, NT, preferred_element_type=F32)
    solve(1, y)
    landed(X2, xs.at[0, 0])
    for w in range(WAVES - 1):
        for b in range(WB):
            out[w * WB + b] = xs[w, b]

    sent(INV_OUT, outer_view)
    sent(INV_IN, inner_view)
    sent(LEAF_RS, own.at[most])
    sent(MAT_RS, mat_rs.at[pl.ds(0, inner * nt - 1)])
    sent(LEAF_AG, leaf_ag.at[most])
    sent(MAT_ZRS, mat_recv.at[pl.ds(0, outer - 1)])
    sent(MAT_ZAG, mat_sum.at[:, pl.ds(0, outer - 1)])
    sent(MAT_AG, mat_ag.at[pl.ds(0, inner * nt - 1)])
    for w in range(WAVES - 1):
        sent(US + w, u_other.at[w])
        sent(UP + w, u_recv.at[w, most])
        sent(X1 + w, xs.at[0, 0])


def fast_body(n, nt, tiles, tile_src, tile_dst, leaf_rhs, leaf_inv, leaf_owner, anc_rhs, anc_inv, anc_owner):
    depth, count = leaf_rhs.shape[-2:]
    kinds = tiles.shape[2]
    ch, share, every = depth // n, count // n, n * nt
    waves = WAVES - 1
    inner = 1
    while inner * inner * 4 <= n and n % (inner * 2) == 0:
        inner *= 2
    outer, part = n // inner, depth // (inner * nt)
    phases = 19
    any_spec = pl.BlockSpec(memory_space=pl.ANY)
    smem = pl.BlockSpec(memory_space=pltpu.SMEM)
    found = pl.pallas_call(
        functools.partial(kernel, n, nt),
        out_shape=pltpu.VMEM((waves * WB, share, depth), BF16),
        in_specs=[any_spec, smem, smem, any_spec, any_spec, smem, any_spec, any_spec, smem],
        out_specs=pl.BlockSpec(memory_space=pltpu.VMEM),
        scratch_shapes=[
            pltpu.VMEM((kinds, depth, depth), BF16),
            pltpu.VMEM((depth, count), BF16),
            pltpu.VMEM((depth, depth), BF16),
            pltpu.VMEM((depth, count), BF16),
            pltpu.VMEM((depth, depth), BF16),
            pltpu.VMEM((n, share + ch // nt, depth), BF16),
            pltpu.VMEM((n, share + ch // nt, depth), BF16),
            pltpu.VMEM((n, WB, share, depth), BF16),
            pltpu.VMEM((WB, waves, ch, depth // nt), BF16),
            pltpu.VMEM((waves, n, ch, depth), BF16),
            pltpu.VMEM((WB * waves, count, depth), BF16),
            pltpu.VMEM((waves, n, share, depth), BF16),
            pltpu.VMEM((waves, n, share, depth), BF16),
            pltpu.VMEM((waves, WB, share, depth), BF16),
            pltpu.VMEM((waves, WB, count, depth), BF16),
            pltpu.VMEM((waves, count, depth), BF16),
            pltpu.VMEM((inner * nt, TW * part + TW * WB * WB, depth), BF16),
            pltpu.VMEM((inner * nt, TW * part + TW * WB * WB, depth), BF16),
            pltpu.VMEM((outer, WB, WB, part // outer, depth), BF16),
            pltpu.VMEM((outer, WB, WB, part // outer, depth), BF16),
            pltpu.VMEM((WB, outer, WB, part // outer, depth), BF16),
            pltpu.VMEM((inner * nt, outer, WB, part // outer, depth), BF16),
            pltpu.SemaphoreType.DMA((5,)),
            pltpu.SemaphoreType.DMA((phases,)),
            pltpu.SemaphoreType.DMA((phases,)),
        ],
        compiler_params=pltpu.CompilerParams(collective_id=0, has_side_effects=True),
    )(tiles, tile_src, tile_dst, leaf_rhs, leaf_inv, leaf_owner, anc_rhs, anc_inv, anc_owner)
    return jnp.swapaxes(found, 1, 2)


def solution(mesh):
    n, nt = mesh.shape["rows"], mesh.shape["trees"]
    placed = (
        P("trees", "rows", None, None, None),
        P("trees", "rows", None),
        P("trees", "rows", None),
        P("trees", "rows", None, None),
        P("trees", "rows", None, None),
        P("trees", None),
        P("trees", "rows", None, None),
        P("rows", None, None),
        P(),
    )

    def body(*args):
        depth, count = args[3].shape[-2:]
        if WAVES == 3 and nt == WB and n > 7 and depth % (16 * n) == 0 and depth % (128 * nt) == 0 and count % (8 * n) == 0:
            return fast_body(n, nt, *args)
        return general_body(*args)

    return jax.shard_map(
        body, mesh=mesh, in_specs=placed, out_specs=P(None, None, "rows"), check_vma=False
    )
```

```python
import functools

import jax
import jax.numpy as jnp
from jax import lax
from jax.experimental import pallas as pl
from jax.experimental.pallas import tpu as pltpu
from jax.sharding import PartitionSpec as P

WAVES = 3
WB = 2
TW = 2
MESH = pl.DeviceIdType.MESH
F32 = jnp.float32
BF16 = jnp.bfloat16


def broadcast(block, axis, source):
    block = jnp.where(lax.axis_index(axis) == source, block, jnp.zeros_like(block))
    return lax.psum(block, axis)


def general_body(tiles, tile_src, tile_dst, leaf_rhs, leaf_inv, leaf_owner, anc_rhs, anc_inv, anc_owner):
    row_count = lax.axis_size("rows")
    here = lax.axis_index("rows")
    share = leaf_rhs.shape[-1] // row_count
    own_leaf = jnp.dot(leaf_inv[0, 0], leaf_rhs[0, 0], preferred_element_type=F32).astype(BF16)
    known = []
    for block in range(WB):
        known.append(broadcast(own_leaf, "rows", leaf_owner[0, block]))
    outputs = []
    for wave in range(1, WAVES):
        start = (wave - 1) * TW
        sources = jnp.stack(known)
        block_tiles = tiles[0, 0, start : start + TW]
        picked = jnp.take(sources, tile_src[0, 0, start : start + TW], axis=0)
        product = jnp.einsum("kij,kjr->kir", block_tiles, picked, preferred_element_type=F32)
        onehot = (
            tile_dst[0, 0, start : start + TW][:, None] == jnp.arange(WB, dtype=jnp.int32)[None, :]
        ).astype(F32)
        owners = anc_owner[(wave - 1) * WB : wave * WB]
        mine = (owners == here).astype(F32)
        partial_value = mine[:, None, None] * anc_rhs[0, 0].astype(F32)[None] - jnp.einsum(
            "kb,kir->bir", onehot, product
        )
        summed = lax.psum(partial_value, ("rows", "trees"))
        chosen = jnp.einsum("b,bir->ir", mine, summed).astype(BF16)
        local_x = jnp.dot(anc_inv[0], chosen, preferred_element_type=F32).astype(BF16)
        for block in range(WB):
            result = broadcast(local_x, "rows", owners[block])
            known.append(result)
            outputs.append(lax.dynamic_slice_in_dim(result, here * share, share, 1))
    return jnp.stack(outputs)


NT = (((1,), (1,)), ((), ()))


def kernel(
    n, nt, tiles_h, src, dst, rhs_h, linv_h, lown, arhs_h, ainv_h, aown, out,
    tiles, rhs, linv, arhs, ainv, own, leaf_rs, leaf_ag, inv_src, inv_rs, inv_half, inv_ag, known, u_send, u_recv, xs,
    u_mine, u_other, mat_src, mat_rs, mat_send, mat_recv, mat_sum, mat_ag, lsem, ssem, rsem,
):
    r = lax.axis_index("rows")
    t = lax.axis_index("trees")
    depth = rhs.shape[0]
    count = rhs.shape[1]
    ch = depth // n
    share = count // n
    every = n * nt

    def partner(m):
        if n & (n - 1):
            return lax.rem(r + m, n)
        j = r
        bit = 1
        while bit < n:
            if m & bit:
                j = j + bit * (1 - 2 * lax.rem(r // bit, 2))
            bit *= 2
        return j

    inner = 1
    while inner * inner * 4 <= n and n % (inner * 2) == 0:
        inner *= 2
    masks = sorted(range(1, n), key=lambda m: (-(m // inner + m % inner), m // inner))
    others = [partner(m) for m in masks]
    everyone = [(j, q) for j in others for q in (t, 1 - t)] + [(r, 1 - t)]

    barrier = pltpu.get_barrier_semaphore()
    for where in everyone:
        pl.semaphore_signal(barrier, inc=1, device_id=where, device_id_type=MESH)

    loads = []
    for i, (a, b) in enumerate(
        ((linv_h.at[0, 0], linv), (rhs_h.at[0, 0], rhs), (ainv_h.at[0], ainv), (arhs_h.at[0, 0], arhs), (tiles_h.at[0, 0], tiles))
    ):
        c = pltpu.make_async_copy(a, b, lsem.at[i])
        c.start()
        loads.append(c)
    coef = []
    for k in range(TW):
        for b in range(WB):
            for s in range(WB):
                hit = (dst[0, 0, TW + k] == b) & (src[0, 0, TW + k] == WB + s)
                coef.append(jnp.full((1, depth), jnp.where(hit, 1.0, 0.0), F32))
    coef = jnp.concatenate(coef, axis=0).astype(BF16)
    loads[0].wait()
    loads[1].wait()
    own_leaf = jnp.dot(linv[...], rhs[...], preferred_element_type=F32)
    own[...] = own_leaf.T.astype(BF16).reshape(n, share, depth)
    pl.semaphore_wait(barrier, every - 1)

    def push(phase, a, b, where):
        pltpu.make_async_remote_copy(
            src_ref=a, dst_ref=b, send_sem=ssem.at[phase], recv_sem=rsem.at[phase],
            device_id=where, device_id_type=MESH,
        ).start()

    def rows_send(phase, make):
        for j in others:
            push(phase, *make(j), (j, t))

    def landed(phase, view):
        pltpu.make_async_copy(view, view, rsem.at[phase]).wait()

    def sent(phase, view):
        pltpu.make_async_copy(view, view, ssem.at[phase]).wait()

    most = pl.ds(0, n - 1)
    outer = n // inner
    ro, ri = r // inner, lax.rem(r, inner)
    chunk = ri * outer + ro
    lanes_each = depth // nt
    lanes = pl.ds(pl.multiple_of(t * lanes_each, lanes_each), lanes_each)

    def rows_of(at):
        return pl.ds(pl.multiple_of(at * ch, ch), ch)

    def inv_part(j):
        return rows_of(lax.rem(j, inner) * outer + j // inner)

    inner_view = inv_ag.at[:, pl.ds(0, (inner - 1) * outer)]
    outer_view = inv_ag.at[0, pl.ds(0, outer * nt - 1)]
    (LEAF_RS, INV_RS, LEAF_AG, INV_OUT, _, INV_SWAP, COEF, MAT_RS, MAT_ZRS, MAT_ZAG, MAT_AG, X1, X2, INV_IN, _,
     UP, _, US, _) = range(19)
    def flip(v, m, size):
        if size & (size - 1):
            return lax.rem(v + m, size)
        j = v
        bit = 1
        while bit < size:
            if m & bit:
                j = j + bit * (1 - 2 * lax.rem(v // bit, 2))
            bit *= 2
        return j

    zs = [flip(ro, m, outer) for m in range(outer - 1, 0, -1)]
    mates = [flip(ri, m, inner) for m in sorted(range(1, inner), key=lambda m: -bin(m).count('1'))]
    near = [(i, q) for i in mates for q in (t, 1 - t)] + [(ri, 1 - t)]
    place = ri * nt + t
    pieces = inner * nt
    part = depth // pieces
    piece = part // outer
    rows_send(LEAF_RS, lambda j: (own.at[j], leaf_rs.at[r]))
    leaf_rs[r] = own[r]
    loads[2].wait()
    half, width = ch // nt, depth // nt
    lanes0 = pl.ds(pl.multiple_of(t * width, width), width)
    mine = ainv[:, lanes0]
    for j in range(n):
        at = (j % inner) * (n // inner) + j // inner
        inv_src[j] = mine[at * ch : (at + 1) * ch]
    rows_send(INV_RS, lambda j: (inv_src.at[j], inv_rs.at[r]))
    inv_rs[r] = inv_src[r]
    loads[4].wait()
    pieces = inner * nt
    part = depth // pieces
    for j in range(pieces):
        for k in range(TW):
            mat_src[j, k * part : (k + 1) * part] = tiles[TW + k, j * part : (j + 1) * part]
        mat_src[j, TW * part :] = coef
    for i, q in near:
        push(MAT_RS, mat_src.at[i * nt + q], mat_rs.at[place], (ro * inner + i, q))
    mat_rs[place] = mat_src[place]
    landed(LEAF_RS, leaf_rs.at[most])
    for b in range(WB):
        leaf_ag[r, b] = leaf_rs[lown[0, b]]
    rows_send(LEAF_AG, lambda j: (leaf_ag.at[r], leaf_ag.at[r]))

    landed(INV_RS, inv_rs.at[most])
    for b in range(WB):
        for w in range(WAVES - 1):
            inv_half[b, w] = inv_rs[aown[w * WB + b]]
    for z in zs:
        for q in (t, 1 - t):
            push(INV_OUT, inv_half.at[q], inv_ag.at[:, chunk, :, lanes], (z * inner + ri, q))
    push(INV_OUT, inv_half.at[1 - t], inv_ag.at[:, chunk, :, lanes], (r, 1 - t))
    inv_ag[:, chunk, :, lanes] = inv_half[t]
    landed(MAT_RS, mat_rs.at[pl.ds(0, inner * nt - 1)])
    slots = [[jnp.zeros((part, depth), F32) for s in range(WB)] for b in range(WB)]
    for j in range(inner * nt):
        scales = mat_rs[j, TW * part :].astype(F32)
        for k in range(TW):
            value = mat_rs[j, k * part : (k + 1) * part].astype(F32)
            for b in range(WB):
                for s in range(WB):
                    at = (k * WB + b) * WB + s
                    slots[b][s] = slots[b][s] + scales[at : at + 1] * value
    for b in range(WB):
        for s in range(WB):
            mat_send[:, b, s] = slots[b][s].reshape(outer, piece, depth).astype(BF16)
    for z in zs:
        push(MAT_ZRS, mat_send.at[z], mat_recv.at[ro], (z * inner + ri, t))
    mat_recv[ro] = mat_send[ro]

    loads[3].wait()
    arhs_t = arhs[...].astype(F32).T
    landed(MAT_ZRS, mat_recv.at[pl.ds(0, outer - 1)])
    mat_sum[:, ro] = jnp.sum(mat_recv[...].astype(F32), axis=0).astype(BF16)
    for z in zs:
        push(MAT_ZAG, mat_sum.at[:, ro], mat_sum.at[:, ro], (z * inner + ri, t))

    landed(LEAF_AG, leaf_ag.at[most])
    for b in range(WB):
        known[b] = leaf_ag[:, b].reshape(count, depth)
    landed(INV_OUT, outer_view)
    held = pl.ds(ri * outer, outer)
    for i in mates:
        push(INV_IN, inv_ag.at[:, held], inv_ag.at[:, held], (ro * inner + i, t))
    for w in (0,):
        products = []
        for k in range(w * TW, (w + 1) * TW):
            from_leaf = known[jnp.minimum(src[0, 0, k], WB - 1)]
            products.append(lax.dot_general(from_leaf, tiles[k], NT, preferred_element_type=F32))
        for b in range(WB):
            u = jnp.where(aown[w * WB + b] == r, arhs_t, 0.0)
            for k in range(TW):
                hit = (dst[0, 0, w * TW + k] == b) & (src[0, 0, w * TW + k] < WB)
                u = u - jnp.where(hit, products[k], 0.0)
            u_mine[w, b] = u.astype(BF16)
        push(US + w, u_mine.at[w, 1 - t], u_other.at[w], (r, 1 - t))
    for w in (1,):
        products = []
        for k in range(w * TW, (w + 1) * TW):
            from_leaf = known[jnp.minimum(src[0, 0, k], WB - 1)]
            products.append(lax.dot_general(from_leaf, tiles[k], NT, preferred_element_type=F32))
        for b in range(WB):
            u = jnp.where(aown[w * WB + b] == r, arhs_t, 0.0)
            for k in range(TW):
                hit = (dst[0, 0, w * TW + k] == b) & (src[0, 0, w * TW + k] < WB)
                u = u - jnp.where(hit, products[k], 0.0)
            u_mine[w, b] = u.astype(BF16)
        push(US + w, u_mine.at[w, 1 - t], u_other.at[w], (r, 1 - t))
    for w in (0,):
        landed(US + w, u_other.at[w])
        u = u_mine[w, t].astype(F32) + u_other[w].astype(F32)
        u_send[w] = u.reshape(n, share, depth).astype(BF16)
        rows_send(UP + w, lambda j: (u_send.at[w, j], u_recv.at[w, r]))
        u_recv[w, r] = u_send[w, r]
    for w in (1,):
        landed(US + w, u_other.at[w])
        u = u_mine[w, t].astype(F32) + u_other[w].astype(F32)
        u_send[w] = u.reshape(n, share, depth).astype(BF16)
        rows_send(UP + w, lambda j: (u_send.at[w, j], u_recv.at[w, r]))
        u_recv[w, r] = u_send[w, r]
    landed(MAT_ZAG, mat_sum.at[:, pl.ds(0, outer - 1)])
    for i, q in near:
        push(MAT_AG, mat_sum.at[q], mat_ag.at[place], (ro * inner + i, q))
    mat_ag[place] = mat_sum[t]
    def solve(w, y):
        inv = inv_ag[w].reshape(depth, depth)
        xs[w, t] = lax.dot_general(y.astype(BF16), inv, NT, preferred_element_type=F32).astype(BF16)
        push(X1 + w, xs.at[w, t], xs.at[w, t], (r, 1 - t))

    landed(UP, u_recv.at[0, most])
    y = jnp.sum(u_recv[0].astype(F32), axis=0)
    landed(INV_IN, inner_view)
    solve(0, y)
    landed(UP + 1, u_recv.at[1, most])
    y = jnp.sum(u_recv[1].astype(F32), axis=0)
    landed(MAT_AG, mat_ag.at[pl.ds(0, inner * nt - 1)])
    landed(X1, xs.at[0, 0])
    for s in range(WB):
        mat = mat_ag[:, :, s].reshape(depth, depth)
        y = y - lax.dot_general(xs[0, s], mat, NT, preferred_element_type=F32)
    solve(1, y)
    landed(X2, xs.at[0, 0])
    for w in range(WAVES - 1):
        for b in range(WB):
            out[w * WB + b] = xs[w, b]

    sent(INV_OUT, outer_view)
    sent(INV_IN, inner_view)
    sent(INV_RS, inv_rs.at[most])
    sent(LEAF_RS, own.at[most])
    sent(MAT_RS, mat_rs.at[pl.ds(0, inner * nt - 1)])
    sent(LEAF_AG, leaf_ag.at[most])
    sent(MAT_ZRS, mat_recv.at[pl.ds(0, outer - 1)])
    sent(MAT_ZAG, mat_sum.at[:, pl.ds(0, outer - 1)])
    sent(MAT_AG, mat_ag.at[pl.ds(0, inner * nt - 1)])
    for w in range(WAVES - 1):
        sent(US + w, u_other.at[w])
        sent(UP + w, u_recv.at[w, most])
        sent(X1 + w, xs.at[0, 0])


def fast_body(n, nt, tiles, tile_src, tile_dst, leaf_rhs, leaf_inv, leaf_owner, anc_rhs, anc_inv, anc_owner):
    depth, count = leaf_rhs.shape[-2:]
    kinds = tiles.shape[2]
    ch, share, every = depth // n, count // n, n * nt
    waves = WAVES - 1
    inner = 1
    while inner * inner * 4 <= n and n % (inner * 2) == 0:
        inner *= 2
    outer, part = n // inner, depth // (inner * nt)
    phases = 19
    any_spec = pl.BlockSpec(memory_space=pl.ANY)
    smem = pl.BlockSpec(memory_space=pltpu.SMEM)
    found = pl.pallas_call(
        functools.partial(kernel, n, nt),
        out_shape=pltpu.VMEM((waves * WB, share, depth), BF16),
        in_specs=[any_spec, smem, smem, any_spec, any_spec, smem, any_spec, any_spec, smem],
        out_specs=pl.BlockSpec(memory_space=pltpu.VMEM),
        scratch_shapes=[
            pltpu.VMEM((kinds, depth, depth), BF16),
            pltpu.VMEM((depth, count), BF16),
            pltpu.VMEM((depth, depth), BF16),
            pltpu.VMEM((depth, count), BF16),
            pltpu.VMEM((depth, depth), BF16),
            pltpu.VMEM((n, share, depth), BF16),
            pltpu.VMEM((n, share, depth), BF16),
            pltpu.VMEM((n, WB, share, depth), BF16),
            pltpu.VMEM((n, ch, depth // nt), BF16),
            pltpu.VMEM((n, ch, depth // nt), BF16),
            pltpu.VMEM((WB, waves, ch, depth // nt), BF16),
            pltpu.VMEM((waves, n, ch, depth), BF16),
            pltpu.VMEM((WB * waves, count, depth), BF16),
            pltpu.VMEM((waves, n, share, depth), BF16),
            pltpu.VMEM((waves, n, share, depth), BF16),
            pltpu.VMEM((waves, WB, share, depth), BF16),
            pltpu.VMEM((waves, WB, count, depth), BF16),
            pltpu.VMEM((waves, count, depth), BF16),
            pltpu.VMEM((inner * nt, TW * part + TW * WB * WB, depth), BF16),
            pltpu.VMEM((inner * nt, TW * part + TW * WB * WB, depth), BF16),
            pltpu.VMEM((outer, WB, WB, part // outer, depth), BF16),
            pltpu.VMEM((outer, WB, WB, part // outer, depth), BF16),
            pltpu.VMEM((WB, outer, WB, part // outer, depth), BF16),
            pltpu.VMEM((inner * nt, outer, WB, part // outer, depth), BF16),
            pltpu.SemaphoreType.DMA((5,)),
            pltpu.SemaphoreType.DMA((phases,)),
            pltpu.SemaphoreType.DMA((phases,)),
        ],
        compiler_params=pltpu.CompilerParams(collective_id=0, has_side_effects=True),
    )(tiles, tile_src, tile_dst, leaf_rhs, leaf_inv, leaf_owner, anc_rhs, anc_inv, anc_owner)
    return jnp.swapaxes(found, 1, 2)


def solution(mesh):
    n, nt = mesh.shape["rows"], mesh.shape["trees"]
    placed = (
        P("trees", "rows", None, None, None),
        P("trees", "rows", None),
        P("trees", "rows", None),
        P("trees", "rows", None, None),
        P("trees", "rows", None, None),
        P("trees", None),
        P("trees", "rows", None, None),
        P("rows", None, None),
        P(),
    )

    def body(*args):
        depth, count = args[3].shape[-2:]
        if WAVES == 3 and nt == WB and n > 7 and depth % (16 * n) == 0 and depth % (128 * nt) == 0 and count % (8 * n) == 0:
            return fast_body(n, nt, *args)
        return general_body(*args)

    return jax.shard_map(
        body, mesh=mesh, in_specs=placed, out_specs=P(None, None, "rows"), check_vma=False
    )
```

```python
import functools

import jax
import jax.numpy as jnp
from jax import lax
from jax.experimental import pallas as pl
from jax.experimental.pallas import tpu as pltpu
from jax.sharding import PartitionSpec as P

WAVES = 3
WB = 2
TW = 2
MESH = pl.DeviceIdType.MESH
F32 = jnp.float32
BF16 = jnp.bfloat16


def broadcast(block, axis, source):
    block = jnp.where(lax.axis_index(axis) == source, block, jnp.zeros_like(block))
    return lax.psum(block, axis)


def general_body(tiles, tile_src, tile_dst, leaf_rhs, leaf_inv, leaf_owner, anc_rhs, anc_inv, anc_owner):
    row_count = lax.axis_size("rows")
    here = lax.axis_index("rows")
    share = leaf_rhs.shape[-1] // row_count
    own_leaf = jnp.dot(leaf_inv[0, 0], leaf_rhs[0, 0], preferred_element_type=F32).astype(BF16)
    known = []
    for block in range(WB):
        known.append(broadcast(own_leaf, "rows", leaf_owner[0, block]))
    outputs = []
    for wave in range(1, WAVES):
        start = (wave - 1) * TW
        sources = jnp.stack(known)
        block_tiles = tiles[0, 0, start : start + TW]
        picked = jnp.take(sources, tile_src[0, 0, start : start + TW], axis=0)
        product = jnp.einsum("kij,kjr->kir", block_tiles, picked, preferred_element_type=F32)
        onehot = (
            tile_dst[0, 0, start : start + TW][:, None] == jnp.arange(WB, dtype=jnp.int32)[None, :]
        ).astype(F32)
        owners = anc_owner[(wave - 1) * WB : wave * WB]
        mine = (owners == here).astype(F32)
        partial_value = mine[:, None, None] * anc_rhs[0, 0].astype(F32)[None] - jnp.einsum(
            "kb,kir->bir", onehot, product
        )
        summed = lax.psum(partial_value, ("rows", "trees"))
        chosen = jnp.einsum("b,bir->ir", mine, summed).astype(BF16)
        local_x = jnp.dot(anc_inv[0], chosen, preferred_element_type=F32).astype(BF16)
        for block in range(WB):
            result = broadcast(local_x, "rows", owners[block])
            known.append(result)
            outputs.append(lax.dynamic_slice_in_dim(result, here * share, share, 1))
    return jnp.stack(outputs)


NT = (((1,), (1,)), ((), ()))


def kernel(
    n, nt, tiles_h, src, dst, rhs_h, linv_h, lown, arhs_h, ainv_h, aown, out,
    tiles, rhs, linv, arhs, ainv, own, leaf_rs, leaf_ag, inv_src, inv_rs, inv_half, inv_ag, known, u_send, u_recv, xs,
    u_mine, u_other, mat_src, mat_rs, mat_send, mat_recv, mat_sum, mat_ag, lsem, ssem, rsem,
):
    r = lax.axis_index("rows")
    t = lax.axis_index("trees")
    depth = rhs.shape[0]
    count = rhs.shape[1]
    ch = depth // n
    share = count // n
    every = n * nt

    def partner(m):
        if n & (n - 1):
            return lax.rem(r + m, n)
        j = r
        bit = 1
        while bit < n:
            if m & bit:
                j = j + bit * (1 - 2 * lax.rem(r // bit, 2))
            bit *= 2
        return j

    inner = 1
    while inner * inner * 4 <= n and n % (inner * 2) == 0:
        inner *= 2
    masks = sorted(range(1, n), key=lambda m: (-(m // inner + m % inner), m // inner))
    others = [partner(m) for m in masks]
    everyone = [(j, q) for j in others for q in (t, 1 - t)] + [(r, 1 - t)]

    barrier = pltpu.get_barrier_semaphore()
    for where in everyone:
        pl.semaphore_signal(barrier, inc=1, device_id=where, device_id_type=MESH)

    loads = []
    for i, (a, b) in enumerate(
        ((linv_h.at[0, 0], linv), (rhs_h.at[0, 0], rhs), (ainv_h.at[0], ainv), (arhs_h.at[0, 0], arhs), (tiles_h.at[0, 0], tiles))
    ):
        c = pltpu.make_async_copy(a, b, lsem.at[i])
        c.start()
        loads.append(c)
    coef = []
    for k in range(TW):
        for b in range(WB):
            for s in range(WB):
                hit = (dst[0, 0, TW + k] == b) & (src[0, 0, TW + k] == WB + s)
                coef.append(jnp.full((1, depth), jnp.where(hit, 1.0, 0.0), F32))
    coef = jnp.concatenate(coef, axis=0).astype(BF16)
    loads[0].wait()
    loads[1].wait()
    own_leaf = jnp.dot(linv[...], rhs[...], preferred_element_type=F32)
    own[...] = own_leaf.T.astype(BF16).reshape(n, share, depth)
    pl.semaphore_wait(barrier, every - 1)

    def push(phase, a, b, where):
        pltpu.make_async_remote_copy(
            src_ref=a, dst_ref=b, send_sem=ssem.at[phase], recv_sem=rsem.at[phase],
            device_id=where, device_id_type=MESH,
        ).start()

    def rows_send(phase, make):
        for j in others:
            push(phase, *make(j), (j, t))

    def landed(phase, view):
        pltpu.make_async_copy(view, view, rsem.at[phase]).wait()

    def sent(phase, view):
        pltpu.make_async_copy(view, view, ssem.at[phase]).wait()

    most = pl.ds(0, n - 1)
    outer = n // inner
    ro, ri = r // inner, lax.rem(r, inner)
    chunk = ri * outer + ro
    lanes_each = depth // nt
    lanes = pl.ds(pl.multiple_of(t * lanes_each, lanes_each), lanes_each)

    def rows_of(at):
        return pl.ds(pl.multiple_of(at * ch, ch), ch)

    def inv_part(j):
        return rows_of(lax.rem(j, inner) * outer + j // inner)

    in_views = (inv_ag.at[0, pl.ds(0, inner - 1)], inv_ag.at[1, :, pl.ds(0, outer - 1)])
    (LEAF_RS, INV_RS, LEAF_AG, INV_OUT, _, INV_SWAP, COEF, MAT_RS, MAT_ZRS, MAT_ZAG, MAT_AG, X1, X2, INV_IN, _,
     UP, _, US, _) = range(19)
    def flip(v, m, size):
        if size & (size - 1):
            return lax.rem(v + m, size)
        j = v
        bit = 1
        while bit < size:
            if m & bit:
                j = j + bit * (1 - 2 * lax.rem(v // bit, 2))
            bit *= 2
        return j

    zs = [flip(ro, m, outer) for m in range(outer - 1, 0, -1)]
    mates = [flip(ri, m, inner) for m in sorted(range(1, inner), key=lambda m: -bin(m).count('1'))]
    near = [(i, q) for i in mates for q in (t, 1 - t)] + [(ri, 1 - t)]
    place = ri * nt + t
    pieces = inner * nt
    part = depth // pieces
    piece = part // outer
    rows_send(LEAF_RS, lambda j: (own.at[j], leaf_rs.at[r]))
    leaf_rs[r] = own[r]
    loads[2].wait()
    half, width = ch // nt, depth // nt
    lanes0 = pl.ds(pl.multiple_of(t * width, width), width)
    mine = ainv[:, lanes0]
    for j in range(n):
        at = (j % inner) * (n // inner) + j // inner
        inv_src[j] = mine[at * ch : (at + 1) * ch]
    rows_send(INV_RS, lambda j: (inv_src.at[j], inv_rs.at[r]))
    inv_rs[r] = inv_src[r]
    loads[4].wait()
    pieces = inner * nt
    part = depth // pieces
    for j in range(pieces):
        for k in range(TW):
            mat_src[j, k * part : (k + 1) * part] = tiles[TW + k, j * part : (j + 1) * part]
        mat_src[j, TW * part :] = coef
    for i, q in near:
        push(MAT_RS, mat_src.at[i * nt + q], mat_rs.at[place], (ro * inner + i, q))
    mat_rs[place] = mat_src[place]
    landed(LEAF_RS, leaf_rs.at[most])
    for b in range(WB):
        leaf_ag[r, b] = leaf_rs[lown[0, b]]
    rows_send(LEAF_AG, lambda j: (leaf_ag.at[r], leaf_ag.at[r]))

    landed(INV_RS, inv_rs.at[most])
    for b in range(WB):
        for w in range(WAVES - 1):
            inv_half[b, w] = inv_rs[aown[w * WB + b]]
    for z in zs:
        for q in (t, 1 - t):
            push(INV_OUT, inv_half.at[q, 0], inv_ag.at[0, ri, ro, :, lanes], (z * inner + ri, q))
    push(INV_OUT, inv_half.at[1 - t, 0], inv_ag.at[0, ri, ro, :, lanes], (r, 1 - t))
    for i, q in near:
        push(INV_OUT + 1, inv_half.at[q, 1], inv_ag.at[1, ri, ro, :, lanes], (ro * inner + i, q))
    for w in range(WAVES - 1):
        inv_ag[w, ri, ro, :, lanes] = inv_half[t, w]
    landed(MAT_RS, mat_rs.at[pl.ds(0, inner * nt - 1)])
    slots = [[jnp.zeros((part, depth), F32) for s in range(WB)] for b in range(WB)]
    for j in range(inner * nt):
        scales = mat_rs[j, TW * part :].astype(F32)
        for k in range(TW):
            value = mat_rs[j, k * part : (k + 1) * part].astype(F32)
            for b in range(WB):
                for s in range(WB):
                    at = (k * WB + b) * WB + s
                    slots[b][s] = slots[b][s] + scales[at : at + 1] * value
    for b in range(WB):
        for s in range(WB):
            mat_send[:, b, s] = slots[b][s].reshape(outer, piece, depth).astype(BF16)
    for z in zs:
        push(MAT_ZRS, mat_send.at[z], mat_recv.at[ro], (z * inner + ri, t))
    mat_recv[ro] = mat_send[ro]

    loads[3].wait()
    arhs_t = arhs[...].astype(F32).T
    landed(INV_OUT, inv_rs.at[pl.ds(0, outer * nt - 1)])
    for i in mates:
        push(INV_IN, inv_ag.at[0, ri], inv_ag.at[0, ri], (ro * inner + i, t))
    landed(MAT_ZRS, mat_recv.at[pl.ds(0, outer - 1)])
    mat_sum[:, ro] = jnp.sum(mat_recv[...].astype(F32), axis=0).astype(BF16)
    for z in zs:
        push(MAT_ZAG, mat_sum.at[:, ro], mat_sum.at[:, ro], (z * inner + ri, t))

    landed(LEAF_AG, leaf_ag.at[most])
    for b in range(WB):
        known[b] = leaf_ag[:, b].reshape(count, depth)
    for w in (0,):
        products = []
        for k in range(w * TW, (w + 1) * TW):
            from_leaf = known[jnp.minimum(src[0, 0, k], WB - 1)]
            products.append(lax.dot_general(from_leaf, tiles[k], NT, preferred_element_type=F32))
        for b in range(WB):
            u = jnp.where(aown[w * WB + b] == r, arhs_t, 0.0)
            for k in range(TW):
                hit = (dst[0, 0, w * TW + k] == b) & (src[0, 0, w * TW + k] < WB)
                u = u - jnp.where(hit, products[k], 0.0)
            u_mine[w, b] = u.astype(BF16)
        push(US + w, u_mine.at[w, 1 - t], u_other.at[w], (r, 1 - t))
    for w in (1,):
        products = []
        for k in range(w * TW, (w + 1) * TW):
            from_leaf = known[jnp.minimum(src[0, 0, k], WB - 1)]
            products.append(lax.dot_general(from_leaf, tiles[k], NT, preferred_element_type=F32))
        for b in range(WB):
            u = jnp.where(aown[w * WB + b] == r, arhs_t, 0.0)
            for k in range(TW):
                hit = (dst[0, 0, w * TW + k] == b) & (src[0, 0, w * TW + k] < WB)
                u = u - jnp.where(hit, products[k], 0.0)
            u_mine[w, b] = u.astype(BF16)
        push(US + w, u_mine.at[w, 1 - t], u_other.at[w], (r, 1 - t))
    for w in (0,):
        landed(US + w, u_other.at[w])
        u = u_mine[w, t].astype(F32) + u_other[w].astype(F32)
        u_send[w] = u.reshape(n, share, depth).astype(BF16)
        rows_send(UP + w, lambda j: (u_send.at[w, j], u_recv.at[w, r]))
        u_recv[w, r] = u_send[w, r]
    for w in (1,):
        landed(US + w, u_other.at[w])
        u = u_mine[w, t].astype(F32) + u_other[w].astype(F32)
        u_send[w] = u.reshape(n, share, depth).astype(BF16)
        rows_send(UP + w, lambda j: (u_send.at[w, j], u_recv.at[w, r]))
        u_recv[w, r] = u_send[w, r]
    landed(INV_OUT + 1, inv_rs.at[pl.ds(0, inner * nt - 1)])
    for z in zs:
        push(INV_IN + 1, inv_ag.at[1, :, ro], inv_ag.at[1, :, ro], (z * inner + ri, t))
    landed(MAT_ZAG, mat_sum.at[:, pl.ds(0, outer - 1)])
    for i, q in near:
        push(MAT_AG, mat_sum.at[q], mat_ag.at[place], (ro * inner + i, q))
    mat_ag[place] = mat_sum[t]
    def solve(w, y):
        inv = inv_ag[w].reshape(depth, depth)
        xs[w, t] = lax.dot_general(y.astype(BF16), inv, NT, preferred_element_type=F32).astype(BF16)
        push(X1 + w, xs.at[w, t], xs.at[w, t], (r, 1 - t))

    landed(UP, u_recv.at[0, most])
    y = jnp.sum(u_recv[0].astype(F32), axis=0)
    landed(INV_IN, in_views[0])
    solve(0, y)
    landed(UP + 1, u_recv.at[1, most])
    y = jnp.sum(u_recv[1].astype(F32), axis=0)
    landed(MAT_AG, mat_ag.at[pl.ds(0, inner * nt - 1)])
    landed(INV_IN + 1, in_views[1])
    landed(X1, xs.at[0, 0])
    for s in range(WB):
        mat = mat_ag[:, :, s].reshape(depth, depth)
        y = y - lax.dot_general(xs[0, s], mat, NT, preferred_element_type=F32)
    solve(1, y)
    landed(X2, xs.at[0, 0])
    for w in range(WAVES - 1):
        for b in range(WB):
            out[w * WB + b] = xs[w, b]

    sent(INV_OUT, inv_rs.at[pl.ds(0, outer * nt - 1)])
    sent(INV_OUT + 1, inv_rs.at[pl.ds(0, inner * nt - 1)])
    sent(INV_RS, inv_rs.at[most])
    sent(LEAF_RS, own.at[most])
    sent(MAT_RS, mat_rs.at[pl.ds(0, inner * nt - 1)])
    sent(LEAF_AG, leaf_ag.at[most])
    sent(MAT_ZRS, mat_recv.at[pl.ds(0, outer - 1)])
    sent(MAT_ZAG, mat_sum.at[:, pl.ds(0, outer - 1)])
    sent(MAT_AG, mat_ag.at[pl.ds(0, inner * nt - 1)])
    for w in range(WAVES - 1):
        sent(US + w, u_other.at[w])
        sent(UP + w, u_recv.at[w, most])
        sent(INV_IN + w, in_views[w])
        sent(X1 + w, xs.at[0, 0])


def fast_body(n, nt, tiles, tile_src, tile_dst, leaf_rhs, leaf_inv, leaf_owner, anc_rhs, anc_inv, anc_owner):
    depth, count = leaf_rhs.shape[-2:]
    kinds = tiles.shape[2]
    ch, share, every = depth // n, count // n, n * nt
    waves = WAVES - 1
    inner = 1
    while inner * inner * 4 <= n and n % (inner * 2) == 0:
        inner *= 2
    outer, part = n // inner, depth // (inner * nt)
    phases = 19
    any_spec = pl.BlockSpec(memory_space=pl.ANY)
    smem = pl.BlockSpec(memory_space=pltpu.SMEM)
    found = pl.pallas_call(
        functools.partial(kernel, n, nt),
        out_shape=pltpu.VMEM((waves * WB, share, depth), BF16),
        in_specs=[any_spec, smem, smem, any_spec, any_spec, smem, any_spec, any_spec, smem],
        out_specs=pl.BlockSpec(memory_space=pltpu.VMEM),
        scratch_shapes=[
            pltpu.VMEM((kinds, depth, depth), BF16),
            pltpu.VMEM((depth, count), BF16),
            pltpu.VMEM((depth, depth), BF16),
            pltpu.VMEM((depth, count), BF16),
            pltpu.VMEM((depth, depth), BF16),
            pltpu.VMEM((n, share, depth), BF16),
            pltpu.VMEM((n, share, depth), BF16),
            pltpu.VMEM((n, WB, share, depth), BF16),
            pltpu.VMEM((n, ch, depth // nt), BF16),
            pltpu.VMEM((n, ch, depth // nt), BF16),
            pltpu.VMEM((WB, waves, ch, depth // nt), BF16),
            pltpu.VMEM((waves, inner, outer, ch, depth), BF16),
            pltpu.VMEM((WB * waves, count, depth), BF16),
            pltpu.VMEM((waves, n, share, depth), BF16),
            pltpu.VMEM((waves, n, share, depth), BF16),
            pltpu.VMEM((waves, WB, share, depth), BF16),
            pltpu.VMEM((waves, WB, count, depth), BF16),
            pltpu.VMEM((waves, count, depth), BF16),
            pltpu.VMEM((inner * nt, TW * part + TW * WB * WB, depth), BF16),
            pltpu.VMEM((inner * nt, TW * part + TW * WB * WB, depth), BF16),
            pltpu.VMEM((outer, WB, WB, part // outer, depth), BF16),
            pltpu.VMEM((outer, WB, WB, part // outer, depth), BF16),
            pltpu.VMEM((WB, outer, WB, part // outer, depth), BF16),
            pltpu.VMEM((inner * nt, outer, WB, part // outer, depth), BF16),
            pltpu.SemaphoreType.DMA((5,)),
            pltpu.SemaphoreType.DMA((phases,)),
            pltpu.SemaphoreType.DMA((phases,)),
        ],
        compiler_params=pltpu.CompilerParams(collective_id=0, has_side_effects=True),
    )(tiles, tile_src, tile_dst, leaf_rhs, leaf_inv, leaf_owner, anc_rhs, anc_inv, anc_owner)
    return jnp.swapaxes(found, 1, 2)


def solution(mesh):
    n, nt = mesh.shape["rows"], mesh.shape["trees"]
    placed = (
        P("trees", "rows", None, None, None),
        P("trees", "rows", None),
        P("trees", "rows", None),
        P("trees", "rows", None, None),
        P("trees", "rows", None, None),
        P("trees", None),
        P("trees", "rows", None, None),
        P("rows", None, None),
        P(),
    )

    def body(*args):
        depth, count = args[3].shape[-2:]
        if WAVES == 3 and nt == WB and n > 7 and depth % (16 * n) == 0 and depth % (128 * nt) == 0 and count % (8 * n) == 0:
            return fast_body(n, nt, *args)
        return general_body(*args)

    return jax.shard_map(
        body, mesh=mesh, in_specs=placed, out_specs=P(None, None, "rows"), check_vma=False
    )
```
